32 devices in a mesh: section: 4 (over z), tensor: 8 (over y, x, core).
Axes of the slice: x: 2, y: 2, z: 4, core: 2. Of those that a mesh axis runs over, the one named last changes fastest.
Arguments:
- queries: bfloat16 [512, 16384], P('section', 'tensor'), may hold values from -15 to 15
- tree_kv: bfloat16 [512, 2, 1024], P('section'), may hold values from -6 to 6
- cache: bfloat16 [8, 8, 2, 8192, 128], P('section', None, None, 'tensor'), may hold values from -6 to 6
- cache_len: int32 [8], P('section'), may hold values from 1024 to 8192, as said below
- parents: int32 [8, 64], P('section'), may hold values from 0 to 62, as said below
- out_weight: bfloat16 [16384, 16384], P('tensor', 'section'), may hold values from -0.046875 to 0.046875
Outputs:
- projected: float32 [512, 16384], P('tensor', 'section')
The draws below stay inside these ranges and needn't reach their ends.
Inputs may be any that keep to these rules, and one draw needn't show every extreme that they name: `cache_len`: some request holds a full cache of 8192 positions; every request holds at least 1024. parents[r, 0] = 0 for the root; for j >= 1, parents[r, j] < j.
All inputs are finite; a program needn't handle non-finite values.
Results may differ from the reference program's by a relative error of at most 0.0055.
Values may be sent and summed in bfloat16 or wider, within the bound.
No kernel may reach another device: no remote copies, remote signals or barrier semaphores. Data moves between devices by JAX's collectives and lax.ppermute only.
A program may use at most 128 MiB of HBM per device.

```python
import math
import jax
import jax.numpy as jnp
from jax import lax

D = 16384
HEADS = 128
KVH = 8
HD = 128
TREE = 64
CACHE = 8192
REQS = 8
TOKENS = 512


def draw_queries(key, part):
    values = 2.5 * jnp.clip(jax.random.normal(jax.random.fold_in(key, 1), (TOKENS, HEADS * HD), jnp.float32), -6.0, 6.0)
    return values.astype(jnp.bfloat16)


def draw_cache(key, part):
    values = jnp.clip(jax.random.normal(jax.random.fold_in(key, 2), (REQS, KVH, 2, CACHE, HD), jnp.float32), -6.0, 6.0)
    return values.astype(jnp.bfloat16)


def draw_cache_len(key, part):
    lengths = jax.random.randint(jax.random.fold_in(key, 3), (REQS,), CACHE // 8, CACHE + 1)
    chosen = jax.random.randint(jax.random.fold_in(key, 4), (), 0, REQS)
    return jnp.where(jnp.arange(REQS) == chosen, CACHE, lengths).astype(jnp.int32)


def draw_parents(key, part):
    columns = jnp.arange(TREE)
    upper = jnp.maximum(columns, 1)[None, :]
    drawn = jax.random.randint(jax.random.fold_in(key, 5), (REQS, TREE), 0, upper)
    chosen = jax.random.randint(jax.random.fold_in(key, 6), (), 0, REQS)
    last = (jnp.arange(REQS)[:, None] == chosen) & (columns[None, :] == TREE - 1)
    return jnp.where(last, TREE - 2, drawn).astype(jnp.int32)


def level_of(own_key, shape, shards, smallest, high):
    factor_of = 1.0
    for dim, blocks in shards:
        steps = jax.random.uniform(jax.random.fold_in(jax.random.fold_in(own_key, 6), dim), (blocks,), jnp.float32, smallest / len(shards), high / len(shards))
        factor_of = factor_of * jnp.repeat(jnp.exp(steps), shape[dim] // blocks).reshape((-1,) + (1,) * (len(shape) - 1 - dim))
    return factor_of


def bell_draw(stream_key, extent, deviation, most, shards=(), kind=jnp.bfloat16):
    factor_of = level_of(stream_key, extent, shards, -0.22, 0.18) if shards else 1.0
    array = jax.random.normal(stream_key, extent, jnp.float32) * deviation * factor_of
    return jnp.minimum(jnp.maximum(array, -most), most).astype(kind)


def setup_inputs(seed: int = 0) -> dict:
    arg_keys = jax.random.split(jax.random.key(seed), 7)
    queries = draw_queries(jax.random.fold_in(arg_keys[6], 71), 0)
    tree_kv = bell_draw(arg_keys[1], (TOKENS, 2, KVH * HD), 1.0, 6.0, ((0, 4),))
    cache = draw_cache(jax.random.fold_in(arg_keys[6], 71), 0)
    cache_len = draw_cache_len(jax.random.fold_in(arg_keys[6], 71), 0)
    parents = draw_parents(jax.random.fold_in(arg_keys[6], 71), 0)
    out_weight = bell_draw(arg_keys[5], (HEADS * HD, D), (HEADS * HD) ** -0.5, 0.046875, ((0, 8), (1, 4)))
    return dict(queries=queries, tree_kv=tree_kv, cache=cache, cache_len=cache_len, parents=parents, out_weight=out_weight)


NEGATIVE = -1e+30

def tree_reach(parent_rows):
    tree_size = parent_rows.shape[-1]
    places = jnp.arange(tree_size)
    linked = (places[None, None, :] == parent_rows[:, :, None]) & (places[None, :, None] >= 1)
    reached = (linked | (places[:, None] == places[None, :])[None]).astype(jnp.float32)
    for doubling in range(tree_size.bit_length()):
        reached = jnp.minimum(jnp.einsum('rij,rjk->rik', reached, reached, precision=lax.Precision.HIGHEST), 1.0)
    return reached > 0.5

def reference(queries, tree_kv, cache, cache_len, parents, out_weight):
    group = HEADS // KVH
    scale = 1.0 / math.sqrt(HD)
    reached = tree_reach(parents)
    positions = jnp.arange(CACHE)

    def one_request(items):
        block_queries, block_tree, block_cache, length, block_reach = items
        grouped = jnp.transpose(block_queries.reshape(TREE, KVH, group, HD), (1, 0, 2, 3)).astype(jnp.float32)
        tree_keys = jnp.transpose(block_tree[:, 0].reshape(TREE, KVH, HD), (1, 0, 2)).astype(jnp.float32)
        tree_values = jnp.transpose(block_tree[:, 1].reshape(TREE, KVH, HD), (1, 0, 2)).astype(jnp.float32)
        valid = positions < length

        def one_head(head_items):
            head_queries, head_cache, head_keys, head_values = head_items
            cache_keys = head_cache[0].astype(jnp.float32)
            cache_values = head_cache[1].astype(jnp.float32)
            cache_scores = jnp.einsum('tgd,pd->gtp', head_queries, cache_keys) * scale
            cache_scores = jnp.where(valid, cache_scores, NEGATIVE)
            own_scores = jnp.einsum('tgd,sd->gts', head_queries, head_keys) * scale
            own_scores = jnp.where(block_reach[None], own_scores, NEGATIVE)
            largest = jnp.maximum(lax.optimization_barrier(jnp.max(cache_scores, axis=-1)), lax.optimization_barrier(jnp.max(own_scores, axis=-1)))
            cache_weights = jnp.where(valid, jnp.exp(cache_scores - largest[..., None]), 0.0)
            own_weights = jnp.where(block_reach[None], jnp.exp(own_scores - largest[..., None]), 0.0)
            weight_total = lax.optimization_barrier(jnp.sum(cache_weights, axis=-1)) + lax.optimization_barrier(jnp.sum(own_weights, axis=-1))
            cache_rounded = lax.optimization_barrier(cache_weights.astype(jnp.bfloat16)).astype(jnp.float32)
            own_rounded = lax.optimization_barrier(own_weights.astype(jnp.bfloat16)).astype(jnp.float32)
            summed = jnp.einsum('gtp,pd->gtd', cache_rounded, cache_values)
            summed = summed + jnp.einsum('gts,sd->gtd', own_rounded, head_values)
            return summed / weight_total[..., None]
        heads_out = lax.map(one_head, (grouped, block_cache, tree_keys, tree_values))
        return jnp.transpose(heads_out, (2, 0, 1, 3)).reshape(TREE, HEADS * HD).astype(jnp.bfloat16)
    attended = lax.map(one_request, (queries.reshape(REQS, TREE, HEADS * HD), tree_kv.reshape(REQS, TREE, 2, KVH * HD), cache, cache_len, reached))
    attended = attended.reshape(TOKENS, HEADS * HD)
    return jnp.dot(attended, out_weight, preferred_element_type=jnp.float32)
```

```python
import math
from functools import partial

import jax
import jax.numpy as jnp
from jax import lax
from jax.experimental import pallas as pl
from jax.experimental.pallas import tpu as pltpu
from jax.sharding import PartitionSpec as P


CHUNKS = 2
LOG2E = math.log2(math.e)
NEGATIVE = -1e30
STAT_ROWS = 32
f32 = jnp.float32
bf16 = jnp.bfloat16


def reach_kernel(parent_ref, bias_ref):
    requests, tree, width = bias_ref.shape
    for r in range(requests):
        rows = lax.broadcasted_iota(jnp.int32, (tree, tree), 0)
        cols = lax.broadcasted_iota(jnp.int32, (tree, tree), 1)
        linked = ((parent_ref[r] == cols) & (rows >= 1)) | (rows == cols)
        reached = linked.astype(f32)
        for _ in range((tree - 1).bit_length()):
            half = reached.astype(bf16)
            reached = jnp.minimum(jnp.dot(half, half, preferred_element_type=f32), 1.0)
        bias_ref[r] = jnp.full((tree, width), NEGATIVE, f32)
        bias_ref[r, :, :tree] = jnp.where(reached > 0.5, 0.0, NEGATIVE)


def tree_bias(parents, width):
    requests, tree = parents.shape
    return pl.pallas_call(
        reach_kernel,
        out_shape=jax.ShapeDtypeStruct((requests, tree, width), f32),
        name="reach",
    )(parents[:, :, None])


def attend_kernel(info_ref, q_ref, own_ref, got_ref, *rest, scale, with_tree, block):
    if with_tree:
        tree_k_ref, tree_v_ref, bias_ref, out_ref, ks, vs, qs, bs = rest
    else:
        out_ref, ks, vs, qs = rest
    r = pl.program_id(0)
    requests = pl.num_programs(0)
    tokens = q_ref.shape[1]
    hd = ks.shape[1]
    heads = q_ref.shape[2] // hd
    rows = heads * tokens
    span = own_ref.shape[3]
    own_valid = info_ref[3 + r]
    got_valid = info_ref[3 + requests + r]
    lead_own = info_ref[2] == 0

    def place(ref, base, valid):
        @pl.when(valid >= span)
        def _():
            ks[base : base + span] = ref[0, 0, 0]
            vs[base : base + span, :hd] = ref[0, 0, 1]
            vs[base : base + span, hd:] = jnp.ones((span, hd), bf16)

        @pl.when(valid < span)
        def _():
            lead = jnp.where(lead_own, own_ref[0, 0, 0, 0:1].astype(f32), got_ref[0, 0, 0, 0:1].astype(f32))
            live = lax.broadcasted_iota(jnp.int32, (span, hd), 0) < valid
            ks[base : base + span] = jnp.where(live, ref[0, 0, 0].astype(f32), lead).astype(bf16)
            vs[base : base + span, :hd] = jnp.where(live, ref[0, 0, 1].astype(f32), 0.0).astype(bf16)
            vs[base : base + span, hd:] = live.astype(f32).astype(bf16)

    def stack():
        for h in range(heads):
            qs[h * tokens : (h + 1) * tokens] = q_ref[0, :, h * hd : (h + 1) * hd]
        if with_tree:
            for h in range(block // tokens):
                bs[h * tokens : (h + 1) * tokens] = bias_ref[0]

    eye = lax.broadcasted_iota(jnp.int32, (hd, hd), 0) == lax.broadcasted_iota(jnp.int32, (hd, hd), 1)
    nt = (((1,), (1,)), ((), ()))

    def run(use_cache):
        stack()
        stats = []
        for b in range(rows // block):
            q = qs[b * block : (b + 1) * block]
            tops = []
            if use_cache:
                scores = lax.dot_general(q, ks[...], nt, preferred_element_type=f32)
                tops.append(jnp.max(scores, axis=1, keepdims=True))
            if with_tree:
                own_scores = lax.dot_general(q, tree_k_ref[0], nt, preferred_element_type=f32)
                own_scores = own_scores + bs[...]
                tops.append(jnp.max(own_scores, axis=1, keepdims=True))
            top = tops[0] if len(tops) == 1 else jnp.maximum(tops[0], tops[1])
            shift = top * scale
            summed = None
            if use_cache:
                weights = jnp.exp2(scores * scale - shift).astype(bf16)
                summed = jnp.dot(weights, vs[...], preferred_element_type=f32)
            if with_tree:
                own_weights = jnp.exp2(own_scores * scale - shift).astype(bf16)
                own_sum = jnp.dot(own_weights, tree_v_ref[0], preferred_element_type=f32)
                summed = own_sum if summed is None else summed + own_sum
            total = summed[:, hd:]
            out_ref[0, b * block : (b + 1) * block] = (summed[:, :hd] / total).astype(bf16)
            level = shift + jnp.log2(total)
            for g in range(block // hd):
                part = level[g * hd : (g + 1) * hd]
                stats.append(jnp.sum(jnp.where(eye, part, 0.0), axis=0, keepdims=True))
        pad = 8 - len(stats)
        packed = jnp.concatenate(stats + ([jnp.zeros((pad, hd), f32)] if pad else []), axis=0)
        high = packed.astype(bf16)
        rest_ = packed - high.astype(f32)
        mid = rest_.astype(bf16)
        low = rest_ - mid.astype(f32)
        tail = jnp.concatenate([high.astype(f32), mid.astype(f32), low, jnp.zeros((8, hd), f32)], axis=0)
        out_ref[0, rows : rows + STAT_ROWS] = tail.astype(bf16)

    any_valid = jnp.maximum(own_valid, got_valid) > 0

    @pl.when(any_valid)
    def _():
        place(own_ref, 0, own_valid)
        place(got_ref, span, got_valid)
        run(True)

    @pl.when(jnp.logical_not(any_valid))
    def _():
        if with_tree:
            run(False)
        else:
            out_ref[0, :rows] = jnp.zeros((rows, hd), bf16)
            lines = lax.broadcasted_iota(jnp.int32, (STAT_ROWS, hd), 0)
            out_ref[0, rows : rows + STAT_ROWS] = jnp.where(lines < 8, NEGATIVE, 0.0).astype(bf16)


def attend(info, q, cache, got, tree, scale):
    requests, tokens, width = q.shape
    _, _, _, span, hd = cache.shape
    heads = width // hd
    rows = heads * tokens
    block = min(256, rows)
    in_specs = [
        pl.BlockSpec((1, tokens, width), lambda r, info: (r, 0, 0)),
        pl.BlockSpec((1, 1, 2, span, hd), lambda r, info: (r, info[0], 0, 0, 0)),
        pl.BlockSpec((1, 1, 2, span, hd), lambda r, info: (r, info[1], 0, 0, 0)),
    ]
    operands = [q, cache, got]
    scratch = [
        pltpu.VMEM((2 * span, hd), bf16),
        pltpu.VMEM((2 * span, 2 * hd), bf16),
        pltpu.VMEM((rows, hd), bf16),
    ]
    if tree is not None:
        tree_k, tree_v, bias = tree
        in_specs += [
            pl.BlockSpec((1, *tree_k.shape[1:]), lambda r, info: (r, 0, 0)),
            pl.BlockSpec((1, *tree_v.shape[1:]), lambda r, info: (r, 0, 0)),
            pl.BlockSpec((1, *bias.shape[1:]), lambda r, info: (r, 0, 0)),
        ]
        operands += [tree_k, tree_v, bias]
        scratch += [pltpu.VMEM((block, bias.shape[2]), f32)]
    return pl.pallas_call(
        partial(attend_kernel, scale=scale, with_tree=tree is not None, block=block),
        grid_spec=pltpu.PrefetchScalarGridSpec(
            num_scalar_prefetch=1,
            grid=(requests,),
            in_specs=in_specs,
            out_specs=pl.BlockSpec((1, rows + STAT_ROWS, hd), lambda r, info: (r, 0, 0)),
            scratch_shapes=scratch,
        ),
        out_shape=jax.ShapeDtypeStruct((requests, rows + STAT_ROWS, hd), bf16),
        compiler_params=pltpu.CompilerParams(vmem_limit_bytes=40 << 20),
        cost_estimate=pl.CostEstimate(
            flops=requests * rows * 2 * span * hd * 6,
            transcendentals=requests * rows * 2 * span,
            bytes_accessed=requests * (4 * span * hd * 2 + 2 * rows * hd * 2),
        ),
        name="attend_tree" if tree is not None else "attend",
    )(info, *operands)


def combine_kernel(*refs):
    *parts, out_ref = refs
    hd = parts[0].shape[2]
    rows = parts[0].shape[1] - STAT_ROWS
    requests, tokens, _ = out_ref.shape
    eye = lax.broadcasted_iota(jnp.int32, (hd, hd), 0) == lax.broadcasted_iota(jnp.int32, (hd, hd), 1)
    for r in range(requests):
        levels = []
        for part in parts:
            tail = part[r, rows : rows + STAT_ROWS].astype(f32)
            levels.append(tail[0:8] + tail[8:16] + tail[16:24])
        top = levels[0]
        for level in levels[1:]:
            top = jnp.maximum(top, level)
        shares = [jnp.exp2(level - top) for level in levels]
        total = shares[0]
        for share in shares[1:]:
            total = total + share
        shares = [share / total for share in shares]
        for g in range(rows // hd):
            acc = jnp.zeros((hd, hd), f32)
            for part, share in zip(parts, shares):
                line = jnp.broadcast_to(share[g : g + 1], (hd, hd))
                column = jnp.sum(jnp.where(eye, line, 0.0), axis=1, keepdims=True)
                acc = acc + column * part[r, g * hd : (g + 1) * hd].astype(f32)
            acc = acc.astype(bf16)
            for i in range(hd // tokens):
                h = g * (hd // tokens) + i
                out_ref[r, :, h * hd : (h + 1) * hd] = acc[i * tokens : (i + 1) * tokens]


def combine(parts, tokens):
    requests, rows, hd = parts[0].shape
    heads = (rows - STAT_ROWS) // tokens
    return pl.pallas_call(
        combine_kernel,
        out_shape=jax.ShapeDtypeStruct((requests, tokens, heads * hd), bf16),
        compiler_params=pltpu.CompilerParams(vmem_limit_bytes=24 << 20),
        name="combine",
    )(*parts)


def project_kernel(info_ref, *refs, sections):
    xs = refs[:sections]
    w_ref, keep_ref, send_ref, stack = refs[sections:]
    requests, tokens, _ = xs[0].shape
    half = sections * tokens

    @pl.when(pl.program_id(0) == 0)
    def _():
        for d in range(sections):
            for r in range(requests):
                base = pl.multiple_of(info_ref[d * requests + r] * tokens, tokens)
                stack[pl.ds(base, tokens)] = xs[d][r]

    out = jnp.dot(stack[...], w_ref[...], preferred_element_type=f32)
    keep_ref[...] = out[:half].reshape(keep_ref.shape).astype(keep_ref.dtype)
    send_ref[...] = out[half:].reshape(send_ref.shape).astype(send_ref.dtype)


def project(info, blocks, weight, width=512):
    sections = len(blocks)
    requests, tokens, features = blocks[0].shape
    columns = weight.shape[1]
    half = pl.BlockSpec((sections, tokens, width), lambda j, info: (0, 0, j))
    return pl.pallas_call(
        partial(project_kernel, sections=sections),
        grid_spec=pltpu.PrefetchScalarGridSpec(
            num_scalar_prefetch=1,
            grid=(columns // width,),
            in_specs=[pl.BlockSpec((requests, tokens, features), lambda j, info: (0, 0, 0))] * sections
            + [pl.BlockSpec((features, width), lambda j, info: (0, j))],
            out_specs=[half, half],
            scratch_shapes=[pltpu.VMEM((sections * requests * tokens, features), bf16)],
        ),
        out_shape=[jax.ShapeDtypeStruct((sections, tokens, columns), bf16)] * 2,
        compiler_params=pltpu.CompilerParams(vmem_limit_bytes=40 << 20),
        cost_estimate=pl.CostEstimate(
            flops=2 * sections * requests * tokens * features * columns,
            transcendentals=0,
            bytes_accessed=features * columns * 2 + sections * requests * tokens * (features + columns) * 2,
        ),
        name="project",
    )(info, *blocks, weight)


def pairs(size, distance):
    return [(i, i ^ distance) for i in range(size)]


def shards(queries, tree_kv, cache, cache_len, parents, out_weight):
    requests, kv_count, _, span, hd = cache.shape
    tree = parents.shape[1]
    sections = lax.axis_size("section")
    ranks = lax.axis_size("tensor")
    section = lax.axis_index("section")
    rank = lax.axis_index("tensor")
    core = rank % 2
    chip = rank // 2
    chips = ranks // 2
    own_heads = queries.shape[1] // hd
    group = own_heads * ranks // kv_count
    scale = LOG2E / math.sqrt(hd)
    tokens = tree // CHUNKS
    assert requests == 2 and sections == chips and ranks % kv_count == 0 and kv_count % 2 == 0

    if ranks == kv_count:
        sending = cache.reshape(requests, kv_count // 2, 2, 2, span, hd)
        sending = lax.dynamic_index_in_dim(sending, 1 - core, 2, keepdims=False)
    else:
        sending = cache
    got = lax.ppermute(sending, "tensor", pairs(ranks, 1))

    q = queries.reshape(requests, tree, queries.shape[1])
    q_chunks = [q[:, h * tokens : (h + 1) * tokens] for h in range(CHUNKS)]
    asked = [
        [qc] + [lax.ppermute(qc, "tensor", pairs(ranks, 2 * d)) for d in range(1, chips)] for qc in q_chunks
    ]

    bias = tree_bias(parents, hd)
    own_kv = rank * own_heads // group
    tree_pair = lax.dynamic_slice_in_dim(tree_kv, own_kv * hd, hd, 2)
    tree_pair = tree_pair.reshape(requests, tree, 2, hd)
    empty = jnp.zeros((requests, hd - tree, hd), bf16)
    tree_k = jnp.concatenate([tree_pair[:, :, 0], empty], axis=1)
    tree_v = jnp.concatenate([tree_pair[:, :, 1], empty], axis=1)
    tree_v = jnp.concatenate([tree_v, jnp.ones_like(tree_v)], axis=2)

    own_valid = jnp.clip(cache_len - rank * span, 0, span)
    got_valid = jnp.clip(cache_len - (rank ^ 1) * span, 0, span)

    def info_of(d):
        other = chip ^ d
        own_index = (2 * other + core) * own_heads // group
        got_index = other if ranks == kv_count else own_index
        head = jnp.stack([own_index, got_index, core]).astype(jnp.int32)
        return jnp.concatenate([head, own_valid, got_valid]).astype(jnp.int32)

    infos = [info_of(d) for d in range(chips)]
    order = []
    for d in range(sections):
        step = (section ^ d) ^ chip
        for r in range(requests):
            order.append((r ^ core) * sections + step)
    order = jnp.stack(order).astype(jnp.int32)

    pieces = []
    for h in range(CHUNKS):
        tree_args = (tree_k, tree_v, bias[:, h * tokens : (h + 1) * tokens])
        parts = [attend(infos[0], asked[h][0], cache, got, tree_args, scale)]
        for d in range(1, chips):
            part = attend(infos[d], asked[h][d], cache, got, None, scale)
            parts.append(lax.ppermute(part, "tensor", pairs(ranks, 2 * d)))
        attended = combine(parts, tokens)
        blocks = [attended]
        for d in range(1, sections):
            blocks.append(lax.ppermute(attended, "section", pairs(sections, d)))
        keep, send = project(order, blocks, out_weight)
        partner = lax.ppermute(send, "tensor", pairs(ranks, 1))
        summed = keep.astype(f32) + partner.astype(f32)
        out = summed[0]
        narrow = summed[1:].astype(bf16)
        for d in range(1, chips):
            out = out + lax.ppermute(narrow[d - 1], "tensor", pairs(ranks, 2 * d)).astype(f32)
        pieces.append(out)
    return jnp.concatenate(pieces, axis=0)


def solution(mesh):
    in_specs = (
        P("section", "tensor"),
        P("section", None, None),
        P("section", None, None, "tensor", None),
        P("section"),
        P("section", None),
        P("tensor", "section"),
    )
    out_specs = P("tensor", "section")
    return jax.shard_map(shards, mesh=mesh, in_specs=in_specs, out_specs=out_specs, check_vma=False)
```

```python
import math
from functools import partial

import jax
import jax.numpy as jnp
from jax import lax
from jax.experimental import pallas as pl
from jax.experimental.pallas import tpu as pltpu
from jax.sharding import PartitionSpec as P


CHUNKS = 2
LOG2E = math.log2(math.e)
NEGATIVE = -1e30
STAT_ROWS = 32
f32 = jnp.float32
bf16 = jnp.bfloat16


def prep_kernel(place_ref, parent_ref, tree_ref, bias_ref, k_ref, v_ref, *, ratio):
    requests, tree = parent_ref.shape
    wide, hd = k_ref.shape[1:]
    column = pl.multiple_of(place_ref[1] // ratio * hd, hd)
    parents = parent_ref[...]
    for r in range(requests):
        rows = lax.broadcasted_iota(jnp.int32, (tree, tree), 0)
        cols = lax.broadcasted_iota(jnp.int32, (tree, tree), 1)
        linked = ((parents[r : r + 1] == rows) & (cols >= 1)) | (rows == cols)
        reached = linked.astype(f32)
        for _ in range((tree - 1).bit_length()):
            half = reached.astype(bf16)
            reached = jnp.minimum(jnp.dot(half, half, preferred_element_type=f32), 1.0)
        bias_ref[r] = jnp.full((tree, wide), NEGATIVE, f32)
        bias_ref[r, :, :tree] = jnp.where(reached.T > 0.5, 0.0, NEGATIVE)
        for i, ref in enumerate((k_ref, v_ref)):
            ref[r] = jnp.zeros((wide, hd), bf16)
            ref[r, :tree] = tree_ref[r * tree : (r + 1) * tree, i, pl.ds(column, hd)]


def prep(place, parents, tree_kv, hd, ratio):
    requests, tree = parents.shape
    smem = pl.BlockSpec(memory_space=pltpu.SMEM)
    vmem = pl.BlockSpec(memory_space=pltpu.VMEM)
    return pl.pallas_call(
        partial(prep_kernel, ratio=ratio),
        in_specs=[smem, vmem, vmem],
        out_specs=[vmem] * 3,
        out_shape=[
            jax.ShapeDtypeStruct((requests, tree, hd), f32),
            jax.ShapeDtypeStruct((requests, hd, hd), bf16),
            jax.ShapeDtypeStruct((requests, hd, hd), bf16),
        ],
        compiler_params=pltpu.CompilerParams(vmem_limit_bytes=4 << 20),
        name="prep",
    )(place, parents, tree_kv)


def stage_kernel(info_ref, cache_ref, own_ref, send_ref, sems):
    requests, held = own_ref.shape[:2]
    stride = cache_ref.shape[1] // held
    copies = []
    for r in range(requests):
        for k in range(held):
            for i, ref in enumerate((send_ref, own_ref)):
                source = k * stride + (jnp.bitwise_xor(info_ref[1] & 1, 1 - i) if stride > 1 else 0)
                copies.append(pltpu.make_async_copy(cache_ref.at[r, source], ref.at[r, k], sems.at[r, k, i]))
    for copy in copies:
        copy.start()
    for copy in copies:
        copy.wait()


def stage(place, cache, held):
    requests = cache.shape[0]
    shape = (requests, held, *cache.shape[2:])
    vmem = pl.BlockSpec(memory_space=pltpu.VMEM)
    return pl.pallas_call(
        stage_kernel,
        in_specs=[pl.BlockSpec(memory_space=pltpu.SMEM), pl.BlockSpec(memory_space=pltpu.HBM)],
        out_specs=[vmem, vmem],
        out_shape=[pltpu.VMEM(shape, cache.dtype)] * 2,
        scratch_shapes=[pltpu.SemaphoreType.DMA((requests, held, 2))],
        compiler_params=pltpu.CompilerParams(vmem_limit_bytes=20 << 20),
        name="stage",
    )(place, pltpu.with_memory_space_constraint(cache, pltpu.HBM))


def attend_kernel(place_ref, len_ref, q_ref, own_ref, got_ref, *rest, scale, distance, first, block):
    with_tree = distance == 0
    if with_tree:
        tree_k_ref, tree_v_ref, bias_ref, out_ref, qs, bs = rest
    else:
        out_ref, qs = rest
    requests, tokens, width = q_ref.shape
    span, hd = own_ref.shape[3:]
    heads = width // hd
    rows = heads * tokens
    rank = place_ref[1]
    index = jnp.bitwise_xor(rank // 2, distance)
    eye = lax.broadcasted_iota(jnp.int32, (hd, hd), 0) == lax.broadcasted_iota(jnp.int32, (hd, hd), 1)
    nt = (((1,), (1,)), ((), ()))
    places = lax.broadcasted_iota(jnp.int32, (1, span), 1)

    def one_request(r, _):
        length = len_ref[r]
        dead = [
            jnp.where(places < length - at * span, 0.0, NEGATIVE) for at in (rank, jnp.bitwise_xor(rank, 1))
        ]
        for h in range(heads):
            qs[h * tokens : (h + 1) * tokens] = q_ref[r, :, h * hd : (h + 1) * hd]
        if with_tree:
            for h in range(block // tokens):
                bs[h * tokens : (h + 1) * tokens] = bias_ref[r, first : first + tokens]

        def scores_of(b):
            q = qs[b * block : (b + 1) * block]
            found = []
            for ref, mask in zip((own_ref, got_ref), dead):
                part = lax.dot_general(q, ref[r, index, 0], nt, preferred_element_type=f32)
                found.append(part * scale + mask)
            if with_tree:
                part = lax.dot_general(q, tree_k_ref[r], nt, preferred_element_type=f32)
                found.append(part * scale + bs[...])
            return found

        stats = []
        blocks = rows // block
        current = scores_of(0)
        for b in range(blocks):
            following = scores_of(b + 1) if b + 1 < blocks else None
            top = None
            for part in current:
                peak = jnp.max(part, axis=1, keepdims=True)
                top = peak if top is None else jnp.maximum(top, peak)
            values = [own_ref[r, index, 1], got_ref[r, index, 1]]
            if with_tree:
                values.append(tree_v_ref[r])
            both = None
            for part, value in zip(current, values):
                weights = jnp.exp2(part - top).astype(bf16)
                value = jnp.concatenate([value, jnp.ones_like(value)], axis=1)
                product = jnp.dot(weights, value, preferred_element_type=f32)
                both = product if both is None else both + product
            total = both[:, hd:]
            out_ref[r, b * block : (b + 1) * block] = (both[:, :hd] / total).astype(bf16)
            level = top + jnp.log2(total)
            for g in range(block // hd):
                part = level[g * hd : (g + 1) * hd]
                stats.append(jnp.sum(jnp.where(eye, part, 0.0), axis=0, keepdims=True))
            current = following
        pad = 8 - len(stats)
        packed = jnp.concatenate(stats + ([jnp.zeros((pad, hd), f32)] if pad else []), axis=0)
        high = packed.astype(bf16).astype(f32)
        mid = (packed - high).astype(bf16).astype(f32)
        low = packed - high - mid
        tail = jnp.concatenate([high, mid, low, jnp.zeros((8, hd), f32)], axis=0)
        out_ref[r, rows : rows + STAT_ROWS] = tail.astype(bf16)
        return 0

    lax.fori_loop(0, requests, one_request, 0)


def attend(place, lengths, q, own, got, distance, scale, tree=(), first=0):
    requests, tokens, width = q.shape
    span, hd = own.shape[3:]
    heads = width // hd
    rows = heads * tokens
    block = min(256, rows)
    smem = pl.BlockSpec(memory_space=pltpu.SMEM)
    vmem = pl.BlockSpec(memory_space=pltpu.VMEM)
    operands = [q, own, got, *tree]
    scratch = [pltpu.VMEM((rows, hd), bf16)]
    if tree:
        scratch += [pltpu.VMEM((block, tree[2].shape[2]), f32)]
    return pl.pallas_call(
        partial(attend_kernel, scale=scale, distance=distance, first=first, block=block),
        in_specs=[smem, smem] + [vmem] * len(operands),
        out_specs=vmem,
        out_shape=jax.ShapeDtypeStruct((requests, rows + STAT_ROWS, hd), bf16),
        scratch_shapes=scratch,
        compiler_params=pltpu.CompilerParams(vmem_limit_bytes=16 << 20),
        cost_estimate=pl.CostEstimate(
            flops=requests * rows * 2 * span * hd * 8,
            transcendentals=requests * rows * 2 * span,
            bytes_accessed=requests * (4 * span * hd * 2 + 2 * rows * hd * 2),
        ),
        name=f"attend_{distance}",
    )(place, lengths, *operands)


def combine_kernel(*refs):
    *parts, out_ref = refs
    hd = parts[0].shape[2]
    rows = parts[0].shape[1] - STAT_ROWS
    requests, tokens, _ = out_ref.shape
    eye = lax.broadcasted_iota(jnp.int32, (hd, hd), 0) == lax.broadcasted_iota(jnp.int32, (hd, hd), 1)
    for r in range(requests):
        levels = []
        for part in parts:
            tail = part[r, rows : rows + STAT_ROWS].astype(f32)
            levels.append(tail[0:8] + tail[8:16] + tail[16:24])
        top = levels[0]
        for level in levels[1:]:
            top = jnp.maximum(top, level)
        shares = [jnp.exp2(level - top) for level in levels]
        total = shares[0]
        for share in shares[1:]:
            total = total + share
        shares = [share / total for share in shares]
        for g in range(rows // hd):
            acc = jnp.zeros((hd, hd), f32)
            for part, share in zip(parts, shares):
                line = jnp.broadcast_to(share[g : g + 1], (hd, hd))
                column = jnp.sum(jnp.where(eye, line, 0.0), axis=1, keepdims=True)
                acc = acc + column * part[r, g * hd : (g + 1) * hd].astype(f32)
            acc = acc.astype(bf16)
            for i in range(hd // tokens):
                h = g * (hd // tokens) + i
                out_ref[r, :, h * hd : (h + 1) * hd] = acc[i * tokens : (i + 1) * tokens]


def combine(parts, tokens):
    requests, rows, hd = parts[0].shape
    heads = (rows - STAT_ROWS) // tokens
    return pl.pallas_call(
        combine_kernel,
        in_specs=[pl.BlockSpec(memory_space=pltpu.VMEM)] * len(parts),
        out_specs=pl.BlockSpec(memory_space=pltpu.VMEM),
        out_shape=jax.ShapeDtypeStruct((requests, tokens, heads * hd), bf16),
        compiler_params=pltpu.CompilerParams(vmem_limit_bytes=8 << 20),
        name="combine",
    )(*parts)


def project_kernel(place_ref, *refs, sections, width):
    xs = refs[:sections]
    w_ref, keep_ref, send_ref, stack = refs[sections:]
    requests, tokens, _ = xs[0].shape
    half = sections * tokens
    section, rank = place_ref[0], place_ref[1]
    for d in range(sections):
        step = jnp.bitwise_xor(jnp.bitwise_xor(section, d), rank // 2)
        for r in range(requests):
            base = pl.multiple_of((jnp.bitwise_xor(rank & 1, r) * sections + step) * tokens, tokens)
            stack[pl.ds(base, tokens)] = xs[d][r]

    def columns(j, _):
        at = pl.ds(pl.multiple_of(j * width, width), width)
        out = jnp.dot(stack[...], w_ref[:, at], preferred_element_type=f32)
        keep_ref[:, :, at] = out[:half].reshape(sections, tokens, width).astype(keep_ref.dtype)
        send_ref[:, :, at] = out[half:].reshape(sections, tokens, width).astype(send_ref.dtype)
        return 0

    lax.fori_loop(0, w_ref.shape[1] // width, columns, 0)


def project(place, blocks, weight, width=512):
    sections = len(blocks)
    requests, tokens, features = blocks[0].shape
    columns = weight.shape[1]
    vmem = pl.BlockSpec(memory_space=pltpu.VMEM)
    return pl.pallas_call(
        partial(project_kernel, sections=sections, width=width),
        in_specs=[pl.BlockSpec(memory_space=pltpu.SMEM)] + [vmem] * (sections + 1),
        out_specs=[vmem, vmem],
        out_shape=[
            jax.ShapeDtypeStruct((sections, tokens, columns), f32),
            jax.ShapeDtypeStruct((sections, tokens, columns), bf16),
        ],
        scratch_shapes=[pltpu.VMEM((sections * requests * tokens, features), bf16)],
        compiler_params=pltpu.CompilerParams(vmem_limit_bytes=16 << 20),
        cost_estimate=pl.CostEstimate(
            flops=2 * sections * requests * tokens * features * columns,
            transcendentals=0,
            bytes_accessed=features * columns * 2 + sections * requests * tokens * (features + columns) * 2,
        ),
        name="project",
    )(place, *blocks, weight)


def merge_kernel(keep_ref, partner_ref, own_ref, *send_refs):
    for d in range(keep_ref.shape[0]):
        both = keep_ref[d] + partner_ref[d].astype(f32)
        if d == 0:
            own_ref[...] = both
        else:
            send_refs[d - 1][...] = both.astype(bf16)


def merge(keep, partner):
    vmem = pl.BlockSpec(memory_space=pltpu.VMEM)
    count, tokens, columns = keep.shape
    return pl.pallas_call(
        merge_kernel,
        in_specs=[vmem] * 2,
        out_specs=[vmem] * count,
        out_shape=[jax.ShapeDtypeStruct((tokens, columns), f32)]
        + [jax.ShapeDtypeStruct((tokens, columns), bf16)] * (count - 1),
        compiler_params=pltpu.CompilerParams(vmem_limit_bytes=12 << 20),
        name="merge",
    )(keep, partner)


def finish_kernel(*refs, count):
    *ins, out_ref = refs
    tokens = ins[0].shape[0]
    for h in range(len(ins) // count):
        total = ins[h * count][...]
        for ref in ins[h * count + 1 : (h + 1) * count]:
            total = total + ref[...].astype(f32)
        out_ref[h * tokens : (h + 1) * tokens] = total


def finish(groups):
    vmem = pl.BlockSpec(memory_space=pltpu.VMEM)
    tokens, columns = groups[0][0].shape
    flat = [x for group in groups for x in group]
    return pl.pallas_call(
        partial(finish_kernel, count=len(groups[0])),
        in_specs=[vmem] * len(flat),
        out_specs=vmem,
        out_shape=jax.ShapeDtypeStruct((tokens * len(groups), columns), f32),
        compiler_params=pltpu.CompilerParams(vmem_limit_bytes=12 << 20),
        name="finish",
    )(*flat)


def pairs(size, distance):
    return [(i, i ^ distance) for i in range(size)]


def shards(queries, tree_kv, cache, cache_len, parents, out_weight):
    requests, kv_count, _, span, hd = cache.shape
    tree = parents.shape[1]
    sections = lax.axis_size("section")
    ranks = lax.axis_size("tensor")
    chips = ranks // 2
    own_heads = queries.shape[1] // hd
    group = own_heads * ranks // kv_count
    scale = LOG2E / math.sqrt(hd)
    tokens = tree // CHUNKS
    held = kv_count // 2 if ranks == kv_count else kv_count
    assert requests == 2 and sections == chips == held and group % own_heads == 0
    place = jnp.stack([lax.axis_index("section"), lax.axis_index("tensor")]).astype(jnp.int32)

    q = queries.reshape(requests, tree, queries.shape[1])
    asked = []
    for h in range(CHUNKS):
        qc = q[:, h * tokens : (h + 1) * tokens]
        asked.append([qc] + [lax.ppermute(qc, "tensor", pairs(ranks, 2 * d)) for d in range(1, chips)])

    own, sending = stage(place, cache, held)
    got = lax.ppermute(sending, "tensor", pairs(ranks, 1))
    bias, tree_k, tree_v = prep(place, parents, tree_kv, hd, group // own_heads)

    attended = []
    for h in range(CHUNKS):
        parts = []
        for d in range(1, chips):
            part = attend(place, cache_len, asked[h][d], own, got, d, scale)
            parts.append(lax.ppermute(part, "tensor", pairs(ranks, 2 * d)))
        tree_args = (tree_k, tree_v, bias)
        part = attend(place, cache_len, asked[h][0], own, got, 0, scale, tree_args, h * tokens)
        attended.append(combine([part] + parts, tokens))
    gathered = [
        [x] + [lax.ppermute(x, "section", pairs(sections, d)) for d in range(1, sections)] for x in attended
    ]
    weight = pltpu.with_memory_space_constraint(out_weight, pltpu.VMEM)
    groups = []
    for h in range(CHUNKS):
        blocks = gathered[h]
        if h + 1 < CHUNKS:
            *blocks, _ = lax.optimization_barrier((*blocks, attended[h + 1]))
        keep, send = project(place, blocks, weight)
        partner = lax.ppermute(send, "tensor", pairs(ranks, 1))
        mine, *sends = merge(keep, partner)
        groups.append(
            [mine] + [lax.ppermute(x, "tensor", pairs(ranks, 2 * (d + 1))) for d, x in enumerate(sends)]
        )
    return finish(groups)


def solution(mesh):
    in_specs = (
        P("section", "tensor"),
        P("section", None, None),
        P("section", None, None, "tensor", None),
        P("section"),
        P("section", None),
        P("tensor", "section"),
    )
    out_specs = P("tensor", "section")
    return jax.shard_map(shards, mesh=mesh, in_specs=in_specs, out_specs=out_specs, check_vma=False)
```

```python
import math
from functools import partial

import jax
import jax.numpy as jnp
from jax import lax
from jax.experimental import pallas as pl
from jax.experimental.pallas import tpu as pltpu
from jax.sharding import PartitionSpec as P


CHUNKS = 2
PIECES = (1, 2)
LOG2E = math.log2(math.e)
NEGATIVE = -1e30
STAT_ROWS = 32
f32 = jnp.float32
bf16 = jnp.bfloat16


def prep_kernel(place_ref, len_ref, parent_ref, tree_ref, bias_ref, k_ref, v_ref, dead_ref, *, ratio):
    requests, tree = parent_ref.shape
    wide, hd = k_ref.shape[1:]
    column = pl.multiple_of(place_ref[1] // ratio * hd, hd)
    parents = parent_ref[...]
    for r in range(requests):
        rows = lax.broadcasted_iota(jnp.int32, (tree, tree), 0)
        cols = lax.broadcasted_iota(jnp.int32, (tree, tree), 1)
        linked = ((parents[r : r + 1] == rows) & (cols >= 1)) | (rows == cols)
        reached = linked.astype(f32)
        for _ in range((tree - 1).bit_length()):
            half = reached.astype(bf16)
            reached = jnp.minimum(jnp.dot(half, half, preferred_element_type=f32), 1.0)
        bias_ref[r] = jnp.full((tree, wide), NEGATIVE, f32)
        bias_ref[r, :, :tree] = jnp.where(reached.T > 0.5, 0.0, NEGATIVE)
        for i, ref in enumerate((k_ref, v_ref)):
            ref[r] = jnp.zeros((wide, hd), bf16)
            ref[r, :tree] = tree_ref[r * tree : (r + 1) * tree, i, pl.ds(column, hd)]
    span = dead_ref.shape[2]
    first = lax.broadcasted_iota(jnp.int32, (span, hd), 1) == 0
    places = lax.broadcasted_iota(jnp.int32, (span, hd), 0)
    for r in range(requests):
        for i in range(2):
            live = len_ref[r] - jnp.bitwise_xor(place_ref[1], i) * span
            dead_ref[r, i] = jnp.where(first & (places >= live), NEGATIVE, 0.0).astype(bf16)


def prep(place, lengths, parents, tree_kv, span, hd, ratio):
    requests, tree = parents.shape
    smem = pl.BlockSpec(memory_space=pltpu.SMEM)
    vmem = pl.BlockSpec(memory_space=pltpu.VMEM)
    return pl.pallas_call(
        partial(prep_kernel, ratio=ratio),
        in_specs=[smem, smem, vmem, vmem],
        out_specs=[vmem] * 4,
        out_shape=[
            jax.ShapeDtypeStruct((requests, tree, hd), f32),
            jax.ShapeDtypeStruct((requests, hd, hd), bf16),
            jax.ShapeDtypeStruct((requests, hd, hd), bf16),
            jax.ShapeDtypeStruct((requests, 2, span, hd), bf16),
        ],
        compiler_params=pltpu.CompilerParams(vmem_limit_bytes=6 << 20),
        name="prep",
    )(place, lengths, parents, tree_kv)


def stage_kernel(info_ref, cache_ref, own_ref, send_ref, sems):
    requests, held = own_ref.shape[:2]
    stride = cache_ref.shape[1] // held
    copies = []
    for r in range(requests):
        for k in range(held):
            for i, ref in enumerate((send_ref, own_ref)):
                source = k * stride + (jnp.bitwise_xor(info_ref[1] & 1, 1 - i) if stride > 1 else 0)
                copies.append(pltpu.make_async_copy(cache_ref.at[r, source], ref.at[r, k], sems.at[r, k, i]))
    for copy in copies:
        copy.start()
    for copy in copies:
        copy.wait()


def stage(place, cache, held):
    requests = cache.shape[0]
    shape = (requests, held, *cache.shape[2:])
    vmem = pl.BlockSpec(memory_space=pltpu.VMEM)
    return pl.pallas_call(
        stage_kernel,
        in_specs=[pl.BlockSpec(memory_space=pltpu.SMEM), pl.BlockSpec(memory_space=pltpu.HBM)],
        out_specs=[vmem, vmem],
        out_shape=[pltpu.VMEM(shape, cache.dtype)] * 2,
        scratch_shapes=[pltpu.SemaphoreType.DMA((requests, held, 2))],
        compiler_params=pltpu.CompilerParams(vmem_limit_bytes=20 << 20),
        name="stage",
    )(place, pltpu.with_memory_space_constraint(cache, pltpu.HBM))


def attend_kernel(place_ref, q_ref, own_ref, got_ref, dead_ref, *rest, scale, distance, first, block):
    with_tree = distance == 0
    if with_tree:
        tree_k_ref, tree_v_ref, bias_ref, out_ref, qs, bs = rest
    else:
        out_ref, qs = rest
    requests, tokens, width = q_ref.shape
    _, hd = own_ref.shape[3:]
    heads = width // hd
    rows = heads * tokens
    rank = place_ref[1]
    index = jnp.bitwise_xor(rank // 2, distance)
    eye = lax.broadcasted_iota(jnp.int32, (hd, hd), 0) == lax.broadcasted_iota(jnp.int32, (hd, hd), 1)
    nt = (((1,), (1,)), ((), ()))
    marks = (lax.broadcasted_iota(jnp.int32, (block, hd), 1) == 0).astype(f32).astype(bf16)

    def one_request(r, _):
        for h in range(heads):
            qs[h * tokens : (h + 1) * tokens] = q_ref[r, :, h * hd : (h + 1) * hd]
        if with_tree:
            for h in range(block // tokens):
                bs[h * tokens : (h + 1) * tokens] = bias_ref[r, first : first + tokens]

        def scores_of(b):
            q = qs[b * block : (b + 1) * block]
            found = []
            marked = jnp.concatenate([q, marks], axis=1)
            for i, ref in enumerate((own_ref, got_ref)):
                keys = jnp.concatenate([ref[r, index, 0], dead_ref[r, i]], axis=1)
                found.append(lax.dot_general(marked, keys, nt, preferred_element_type=f32))
            if with_tree:
                part = lax.dot_general(q, tree_k_ref[r], nt, preferred_element_type=f32)
                found.append(part + bs[...])
            return found

        stats = []
        blocks = rows // block
        current = scores_of(0)
        for b in range(blocks):
            following = scores_of(b + 1) if b + 1 < blocks else None
            top = None
            for part in current:
                peak = jnp.max(part, axis=1, keepdims=True)
                top = peak if top is None else jnp.maximum(top, peak)
            top = top * scale
            values = [own_ref[r, index, 1], got_ref[r, index, 1]]
            if with_tree:
                values.append(tree_v_ref[r])
            both = None
            for part, value in zip(current, values):
                weights = jnp.exp2(part * scale - top).astype(bf16)
                value = jnp.concatenate([value, jnp.ones_like(value)], axis=1)
                product = jnp.dot(weights, value, preferred_element_type=f32)
                both = product if both is None else both + product
            total = both[:, hd:]
            out_ref[r, b * block : (b + 1) * block] = (both[:, :hd] / total).astype(bf16)
            level = top + jnp.log2(total)
            for g in range(block // hd):
                part = level[g * hd : (g + 1) * hd]
                stats.append(jnp.sum(jnp.where(eye, part, 0.0), axis=0, keepdims=True))
            current = following
        pad = 8 - len(stats)
        packed = jnp.concatenate(stats + ([jnp.zeros((pad, hd), f32)] if pad else []), axis=0)
        high = packed.astype(bf16).astype(f32)
        mid = (packed - high).astype(bf16).astype(f32)
        low = packed - high - mid
        tail = jnp.concatenate([high, mid, low, jnp.zeros((8, hd), f32)], axis=0)
        out_ref[r, rows : rows + STAT_ROWS] = tail.astype(bf16)
        return 0

    lax.fori_loop(0, requests, one_request, 0)


def attend(place, dead, q, own, got, distance, scale, first, tree=()):
    requests, tokens, width = q.shape
    span, hd = own.shape[3:]
    heads = width // hd
    rows = heads * tokens
    block = min(256, rows)
    smem = pl.BlockSpec(memory_space=pltpu.SMEM)
    vmem = pl.BlockSpec(memory_space=pltpu.VMEM)
    operands = [q, own, got, dead, *tree]
    scratch = [pltpu.VMEM((rows, hd), bf16)]
    if tree:
        scratch += [pltpu.VMEM((block, tree[2].shape[2]), f32)]
    return pl.pallas_call(
        partial(attend_kernel, scale=scale, distance=distance, first=first, block=block),
        in_specs=[smem] + [vmem] * len(operands),
        out_specs=vmem,
        out_shape=jax.ShapeDtypeStruct((requests, rows + STAT_ROWS, hd), bf16),
        scratch_shapes=scratch,
        compiler_params=pltpu.CompilerParams(vmem_limit_bytes=16 << 20),
        cost_estimate=pl.CostEstimate(
            flops=requests * rows * 2 * span * hd * 8,
            transcendentals=requests * rows * 2 * span,
            bytes_accessed=requests * (4 * span * hd * 2 + 2 * rows * hd * 2),
        ),
    )(place, *operands)


def combine_kernel(*refs):
    *parts, out_ref = refs
    hd = parts[0].shape[2]
    rows = parts[0].shape[1] - STAT_ROWS
    requests, tokens, _ = out_ref.shape
    eye = lax.broadcasted_iota(jnp.int32, (hd, hd), 0) == lax.broadcasted_iota(jnp.int32, (hd, hd), 1)
    for r in range(requests):
        levels = []
        for part in parts:
            tail = part[r, rows : rows + STAT_ROWS].astype(f32)
            levels.append(tail[0:8] + tail[8:16] + tail[16:24])
        top = levels[0]
        for level in levels[1:]:
            top = jnp.maximum(top, level)
        shares = [jnp.exp2(level - top) for level in levels]
        total = shares[0]
        for share in shares[1:]:
            total = total + share
        shares = [share / total for share in shares]
        for g in range(rows // hd):
            acc = jnp.zeros((hd, hd), f32)
            for part, share in zip(parts, shares):
                line = jnp.broadcast_to(share[g : g + 1], (hd, hd))
                column = jnp.sum(jnp.where(eye, line, 0.0), axis=1, keepdims=True)
                acc = acc + column * part[r, g * hd : (g + 1) * hd].astype(f32)
            acc = acc.astype(bf16)
            for i in range(hd // tokens):
                h = g * (hd // tokens) + i
                out_ref[r, :, h * hd : (h + 1) * hd] = acc[i * tokens : (i + 1) * tokens]


def combine(parts, tokens):
    requests, rows, hd = parts[0].shape
    heads = (rows - STAT_ROWS) // tokens
    return pl.pallas_call(
        combine_kernel,
        in_specs=[pl.BlockSpec(memory_space=pltpu.VMEM)] * len(parts),
        out_specs=pl.BlockSpec(memory_space=pltpu.VMEM),
        out_shape=jax.ShapeDtypeStruct((requests, tokens, heads * hd), bf16),
        compiler_params=pltpu.CompilerParams(vmem_limit_bytes=8 << 20),
        name="combine",
    )(*parts)


def project_kernel(place_ref, *refs, kinds, width, start):
    sections = len(kinds)
    xs = list(refs[: sum(kinds)])
    w_ref, keep_ref, send_ref, stack = refs[sum(kinds) :]
    requests, tokens, _ = xs[0].shape
    half = sections * tokens
    section, rank = place_ref[0], place_ref[1]
    inner = (section > 0) & (section < sections - 1)
    for d, kind in enumerate(kinds):
        step = jnp.bitwise_xor(jnp.bitwise_xor(section, d), rank // 2)

        def put(x):
            for r in range(requests):
                base = pl.multiple_of((jnp.bitwise_xor(rank & 1, r) * sections + step) * tokens, tokens)
                stack[pl.ds(base, tokens)] = x[r]

        if kind == 1:
            put(xs.pop(0))
        else:
            pl.when(inner)(partial(put, xs.pop(0)))
            pl.when(jnp.logical_not(inner))(partial(put, xs.pop(0)))

    def columns(j, _):
        at = pl.ds(pl.multiple_of(j * width, width), width)
        taken = pl.ds(pl.multiple_of(start + j * width, width), width)
        out = jnp.dot(stack[...], w_ref[:, taken], preferred_element_type=f32)
        keep_ref[:, :, at] = out[:half].reshape(sections, tokens, width).astype(keep_ref.dtype)
        send_ref[:, :, at] = out[half:].reshape(sections, tokens, width).astype(send_ref.dtype)
        return 0

    lax.fori_loop(0, keep_ref.shape[2] // width, columns, 0)


def project(place, blocks, weight, start, columns, width=512):
    sections = len(blocks)
    kinds = tuple(len(block) for block in blocks)
    flat = [x for block in blocks for x in block]
    requests, tokens, features = flat[0].shape
    vmem = pl.BlockSpec(memory_space=pltpu.VMEM)
    return pl.pallas_call(
        partial(project_kernel, kinds=kinds, width=width, start=start),
        in_specs=[pl.BlockSpec(memory_space=pltpu.SMEM)] + [vmem] * (len(flat) + 1),
        out_specs=[vmem, vmem],
        out_shape=[
            jax.ShapeDtypeStruct((sections, tokens, columns), f32),
            jax.ShapeDtypeStruct((sections, tokens, columns), bf16),
        ],
        scratch_shapes=[pltpu.VMEM((sections * requests * tokens, features), bf16)],
        compiler_params=pltpu.CompilerParams(vmem_limit_bytes=16 << 20),
        cost_estimate=pl.CostEstimate(
            flops=2 * sections * requests * tokens * features * columns,
            transcendentals=0,
            bytes_accessed=features * columns * 2 + sections * requests * tokens * (features + columns) * 2,
        ),
        name="project",
    )(place, *flat, weight)


def merge_kernel(keep_ref, partner_ref, own_ref, *send_refs):
    for d in range(keep_ref.shape[0]):
        both = keep_ref[d] + partner_ref[d].astype(f32)
        if d == 0:
            own_ref[...] = both
        else:
            send_refs[d - 1][...] = both.astype(bf16)


def merge(keep, partner):
    vmem = pl.BlockSpec(memory_space=pltpu.VMEM)
    count, tokens, columns = keep.shape
    return pl.pallas_call(
        merge_kernel,
        in_specs=[vmem] * 2,
        out_specs=[vmem] * count,
        out_shape=[jax.ShapeDtypeStruct((tokens, columns), f32)]
        + [jax.ShapeDtypeStruct((tokens, columns), bf16)] * (count - 1),
        compiler_params=pltpu.CompilerParams(vmem_limit_bytes=12 << 20),
        name="merge",
    )(keep, partner)


def finish_kernel(*refs, count, corners):
    *ins, out_ref = refs
    for g, (row, column) in enumerate(corners):
        total = ins[g * count][...]
        for ref in ins[g * count + 1 : (g + 1) * count]:
            total = total + ref[...].astype(f32)
        tokens, columns = total.shape
        out_ref[row : row + tokens, column : column + columns] = total


def finish(groups, corners, shape):
    vmem = pl.BlockSpec(memory_space=pltpu.VMEM)
    flat = [x for group in groups for x in group]
    return pl.pallas_call(
        partial(finish_kernel, count=len(groups[0]), corners=corners),
        in_specs=[vmem] * len(flat),
        out_specs=vmem,
        out_shape=jax.ShapeDtypeStruct(shape, f32),
        compiler_params=pltpu.CompilerParams(vmem_limit_bytes=12 << 20),
        name="finish",
    )(*flat)


def pairs(size, distance):
    return [(i, i ^ distance) for i in range(size)]


def shards(queries, tree_kv, cache, cache_len, parents, out_weight):
    requests, kv_count, _, span, hd = cache.shape
    tree = parents.shape[1]
    sections = lax.axis_size("section")
    ranks = lax.axis_size("tensor")
    chips = ranks // 2
    own_heads = queries.shape[1] // hd
    group = own_heads * ranks // kv_count
    scale = LOG2E / math.sqrt(hd)
    tokens = tree // CHUNKS
    held = kv_count // 2 if ranks == kv_count else kv_count
    assert requests == 2 and sections == chips == held and group % own_heads == 0
    place = jnp.stack([lax.axis_index("section"), lax.axis_index("tensor")]).astype(jnp.int32)

    def send(x, axis, size, distance, only=None):
        return lax.ppermute(x, axis, only or pairs(size, distance))

    def along(h, x):
        if sections != 4 or h > 0:
            return [[x]] + [[send(x, "section", sections, d)] for d in range(1, sections)]
        near = send(x, "section", sections, 1)
        middle = send(x, "section", sections, 3, [(1, 2), (2, 1)])
        crossed = send(near, "section", sections, 3, [(1, 2), (2, 1)])
        farthest = send(near, "section", sections, 2, [(1, 3), (2, 0)])
        passed = send(middle, "section", sections, 1, [(1, 0), (2, 3)])
        return [[x], [near], [crossed, passed], [middle, farthest]]

    own, sending = stage(place, cache, held)
    got = send(sending, "tensor", ranks, 1)
    queries = queries.reshape(requests, tree, queries.shape[1])
    asked = []
    for h in range(CHUNKS):
        mine = queries[:, h * tokens : (h + 1) * tokens]
        direct = range(1, chips - 1 if chips == 4 else chips)
        asked.append([mine] + [send(mine, "tensor", ranks, 2 * d) for d in direct])
        if chips == 4:
            via = 1 + h % 2
            asked[h].append(send(asked[h][via], "tensor", ranks, 2 * (3 - via)))
    bias, tree_k, tree_v, dead = prep(place, cache_len, parents, tree_kv, span, hd, group // own_heads)
    weight = pltpu.with_memory_space_constraint(out_weight, pltpu.VMEM)

    gathered = []
    for h in range(CHUNKS):
        parts = []
        for d in range(chips):
            tree_args = () if d else (tree_k, tree_v, bias)
            part = attend(place, dead, asked[h][d], own, got, d, scale, h * tokens, tree_args)
            parts.append(send(part, "tensor", ranks, 2 * d) if d else part)
        attended = combine(parts, tokens)
        gathered.append(along(h, attended))
    groups, corners = [], []
    width = out_weight.shape[1]
    for h in range(CHUNKS):
        columns = width // PIECES[h]
        for c in range(PIECES[h]):
            keep, give = project(place, gathered[h], weight, c * columns, columns)
            partner = send(give, "tensor", ranks, 1)
            mine, *sends = merge(keep, partner)
            groups.append([mine] + [send(x, "tensor", ranks, 2 * (d + 1)) for d, x in enumerate(sends)])
            corners.append((h * tokens, c * columns))
    return finish(groups, tuple(corners), (CHUNKS * tokens, width))


def solution(mesh):
    in_specs = (
        P("section", "tensor"),
        P("section", None, None),
        P("section", None, None, "tensor", None),
        P("section"),
        P("section", None),
        P("tensor", "section"),
    )
    out_specs = P("tensor", "section")
    return jax.shard_map(shards, mesh=mesh, in_specs=in_specs, out_specs=out_specs, check_vma=False)
```

```python
import math
from functools import partial

import jax
import jax.numpy as jnp
from jax import lax
from jax.experimental import pallas as pl
from jax.experimental.pallas import tpu as pltpu
from jax.sharding import PartitionSpec as P


CHUNKS = 2
PIECES = (1, 2)
LOG2E = math.log2(math.e)
NEGATIVE = -1e30
STAT_ROWS = 32
f32 = jnp.float32
bf16 = jnp.bfloat16


def prep_kernel(
    place_ref, len_ref, parent_ref, tree_ref, cache_ref, bias_ref, k_ref, v_ref, dead_ref, own_ref, sems, *, ratio
):
    copies = fetch(place_ref, cache_ref, own_ref, sems, 0)
    requests, tree = parent_ref.shape
    wide, hd = k_ref.shape[1:]
    column = pl.multiple_of(place_ref[1] // ratio * hd, hd)
    parents = parent_ref[...]
    for r in range(requests):
        rows = lax.broadcasted_iota(jnp.int32, (tree, tree), 0)
        cols = lax.broadcasted_iota(jnp.int32, (tree, tree), 1)
        linked = ((parents[r : r + 1] == rows) & (cols >= 1)) | (rows == cols)
        reached = linked.astype(f32)
        for _ in range((tree - 1).bit_length()):
            half = reached.astype(bf16)
            reached = jnp.minimum(jnp.dot(half, half, preferred_element_type=f32), 1.0)
        bias_ref[r] = jnp.full((tree, wide), NEGATIVE, f32)
        bias_ref[r, :, :tree] = jnp.where(reached.T > 0.5, 0.0, NEGATIVE)
        for i, ref in enumerate((k_ref, v_ref)):
            ref[r] = jnp.zeros((wide, hd), bf16)
            ref[r, :tree] = tree_ref[r * tree : (r + 1) * tree, i, pl.ds(column, hd)]
    span = dead_ref.shape[2]
    first = lax.broadcasted_iota(jnp.int32, (span, hd), 1) == 0
    places = lax.broadcasted_iota(jnp.int32, (span, hd), 0)
    for r in range(requests):
        for i in range(2):
            live = len_ref[r] - jnp.bitwise_xor(place_ref[1], i) * span
            dead_ref[r, i] = jnp.where(first & (places >= live), NEGATIVE, 0.0).astype(bf16)
    for copy in copies:
        copy.wait()


def prep(place, lengths, parents, tree_kv, cache, held, ratio):
    requests, tree = parents.shape
    span, hd = cache.shape[3:]
    smem = pl.BlockSpec(memory_space=pltpu.SMEM)
    vmem = pl.BlockSpec(memory_space=pltpu.VMEM)
    return pl.pallas_call(
        partial(prep_kernel, ratio=ratio),
        in_specs=[smem, smem, vmem, vmem, pl.BlockSpec(memory_space=pltpu.HBM)],
        out_specs=[vmem] * 5,
        out_shape=[
            jax.ShapeDtypeStruct((requests, tree, hd), f32),
            jax.ShapeDtypeStruct((requests, hd, hd), bf16),
            jax.ShapeDtypeStruct((requests, hd, hd), bf16),
            jax.ShapeDtypeStruct((requests, 2, span, hd), bf16),
            pltpu.VMEM((requests, held, *cache.shape[2:]), bf16),
        ],
        scratch_shapes=[pltpu.SemaphoreType.DMA((requests, held))],
        compiler_params=pltpu.CompilerParams(vmem_limit_bytes=12 << 20),
        name="prep",
    )(place, lengths, parents, tree_kv, cache)


def fetch(place_ref, cache_ref, to_ref, sems, other):
    requests, held = to_ref.shape[:2]
    stride = cache_ref.shape[1] // held
    copies = []
    for r in range(requests):
        for k in range(held):
            source = k * stride + (jnp.bitwise_xor(place_ref[1] & 1, other) if stride > 1 else 0)
            copies.append(pltpu.make_async_copy(cache_ref.at[r, source], to_ref.at[r, k], sems.at[r, k]))
    for copy in copies:
        copy.start()
    return copies


def stage_kernel(place_ref, cache_ref, send_ref, sems):
    for copy in fetch(place_ref, cache_ref, send_ref, sems, 1):
        copy.wait()


def stage(place, cache, held):
    requests = cache.shape[0]
    return pl.pallas_call(
        stage_kernel,
        in_specs=[pl.BlockSpec(memory_space=pltpu.SMEM), pl.BlockSpec(memory_space=pltpu.HBM)],
        out_specs=pl.BlockSpec(memory_space=pltpu.VMEM),
        out_shape=pltpu.VMEM((requests, held, *cache.shape[2:]), cache.dtype),
        scratch_shapes=[pltpu.SemaphoreType.DMA((requests, held))],
        compiler_params=pltpu.CompilerParams(vmem_limit_bytes=4 << 20),
        name="stage",
    )(place, cache)


def attend_kernel(place_ref, q_ref, own_ref, got_ref, dead_ref, *rest, scale, distance, first, block):
    with_tree = distance == 0
    if with_tree:
        tree_k_ref, tree_v_ref, bias_ref, out_ref, qs, bs = rest
    else:
        out_ref, qs = rest
    requests, tokens, width = q_ref.shape
    _, hd = own_ref.shape[3:]
    heads = width // hd
    rows = heads * tokens
    rank = place_ref[1]
    index = jnp.bitwise_xor(rank // 2, distance)
    eye = lax.broadcasted_iota(jnp.int32, (hd, hd), 0) == lax.broadcasted_iota(jnp.int32, (hd, hd), 1)
    nt = (((1,), (1,)), ((), ()))
    marks = (lax.broadcasted_iota(jnp.int32, (block, hd), 1) == 0).astype(f32).astype(bf16)

    blocks = rows // block
    units = [(r, b) for r in range(requests) for b in range(blocks)]
    for r in range(requests):
        for h in range(heads):
            qs[r, h * tokens : (h + 1) * tokens] = q_ref[r, :, h * hd : (h + 1) * hd]
        if with_tree:
            for h in range(block // tokens):
                bs[r, h * tokens : (h + 1) * tokens] = bias_ref[r, first : first + tokens]

    def scores_of(r, b):
        q = qs[r, b * block : (b + 1) * block]
        found = []
        marked = jnp.concatenate([q, marks], axis=1)
        for i, ref in enumerate((own_ref, got_ref)):
            keys = jnp.concatenate([ref[r, index, 0], dead_ref[r, i]], axis=1)
            found.append(lax.dot_general(marked, keys, nt, preferred_element_type=f32))
        if with_tree:
            part = lax.dot_general(q, tree_k_ref[r], nt, preferred_element_type=f32)
            found.append(part + bs[r])
        return found

    stats = [[] for _ in range(requests)]
    current = scores_of(*units[0])
    for at, (r, b) in enumerate(units):
        following = scores_of(*units[at + 1]) if at + 1 < len(units) else None
        top = None
        for part in current:
            peak = jnp.max(part, axis=1, keepdims=True)
            top = peak if top is None else jnp.maximum(top, peak)
        top = top * scale
        values = [own_ref[r, index, 1], got_ref[r, index, 1]]
        if with_tree:
            values.append(tree_v_ref[r])
        both = None
        for part, value in zip(current, values):
            weights = jnp.exp2(part * scale - top).astype(bf16)
            value = jnp.concatenate([value, jnp.ones_like(value)], axis=1)
            product = jnp.dot(weights, value, preferred_element_type=f32)
            both = product if both is None else both + product
        total = both[:, hd:]
        out_ref[r, b * block : (b + 1) * block] = (both[:, :hd] / total).astype(bf16)
        level = top + jnp.log2(total)
        for g in range(block // hd):
            part = level[g * hd : (g + 1) * hd]
            stats[r].append(jnp.sum(jnp.where(eye, part, 0.0), axis=0, keepdims=True))
        current = following
    for r in range(requests):
        pad = 8 - len(stats[r])
        packed = jnp.concatenate(stats[r] + ([jnp.zeros((pad, hd), f32)] if pad else []), axis=0)
        high = packed.astype(bf16).astype(f32)
        mid = (packed - high).astype(bf16).astype(f32)
        low = packed - high - mid
        tail = jnp.concatenate([high, mid, low, jnp.zeros((8, hd), f32)], axis=0)
        out_ref[r, rows : rows + STAT_ROWS] = tail.astype(bf16)


def attend(place, dead, q, own, got, distance, scale, first, tree=()):
    requests, tokens, width = q.shape
    span, hd = own.shape[3:]
    heads = width // hd
    rows = heads * tokens
    block = min(256, rows)
    smem = pl.BlockSpec(memory_space=pltpu.SMEM)
    vmem = pl.BlockSpec(memory_space=pltpu.VMEM)
    operands = [q, own, got, dead, *tree]
    scratch = [pltpu.VMEM((requests, rows, hd), bf16)]
    if tree:
        scratch += [pltpu.VMEM((requests, block, tree[2].shape[2]), f32)]
    return pl.pallas_call(
        partial(attend_kernel, scale=scale, distance=distance, first=first, block=block),
        in_specs=[smem] + [vmem] * len(operands),
        out_specs=vmem,
        out_shape=jax.ShapeDtypeStruct((requests, rows + STAT_ROWS, hd), bf16),
        scratch_shapes=scratch,
        compiler_params=pltpu.CompilerParams(vmem_limit_bytes=16 << 20),
        cost_estimate=pl.CostEstimate(
            flops=requests * rows * 2 * span * hd * 8,
            transcendentals=requests * rows * 2 * span,
            bytes_accessed=requests * (4 * span * hd * 2 + 2 * rows * hd * 2),
        ),
    )(place, *operands)


def combine_kernel(*refs):
    *parts, out_ref = refs
    hd = parts[0].shape[2]
    rows = parts[0].shape[1] - STAT_ROWS
    requests, tokens, _ = out_ref.shape
    eye = lax.broadcasted_iota(jnp.int32, (hd, hd), 0) == lax.broadcasted_iota(jnp.int32, (hd, hd), 1)
    for r in range(requests):
        levels = []
        for part in parts:
            tail = part[r, rows : rows + STAT_ROWS].astype(f32)
            levels.append(tail[0:8] + tail[8:16] + tail[16:24])
        top = levels[0]
        for level in levels[1:]:
            top = jnp.maximum(top, level)
        shares = [jnp.exp2(level - top) for level in levels]
        total = shares[0]
        for share in shares[1:]:
            total = total + share
        shares = [share / total for share in shares]
        for g in range(rows // hd):
            acc = jnp.zeros((hd, hd), f32)
            for part, share in zip(parts, shares):
                line = jnp.broadcast_to(share[g : g + 1], (hd, hd))
                column = jnp.sum(jnp.where(eye, line, 0.0), axis=1, keepdims=True)
                acc = acc + column * part[r, g * hd : (g + 1) * hd].astype(f32)
            acc = acc.astype(bf16)
            for i in range(hd // tokens):
                h = g * (hd // tokens) + i
                out_ref[r, :, h * hd : (h + 1) * hd] = acc[i * tokens : (i + 1) * tokens]


def combine(parts, tokens):
    requests, rows, hd = parts[0].shape
    heads = (rows - STAT_ROWS) // tokens
    return pl.pallas_call(
        combine_kernel,
        in_specs=[pl.BlockSpec(memory_space=pltpu.VMEM)] * len(parts),
        out_specs=pl.BlockSpec(memory_space=pltpu.VMEM),
        out_shape=jax.ShapeDtypeStruct((requests, tokens, heads * hd), bf16),
        compiler_params=pltpu.CompilerParams(vmem_limit_bytes=8 << 20),
        name="combine",
    )(*parts)


def project_kernel(place_ref, *refs, kinds, width, start):
    sections = len(kinds)
    xs = list(refs[: sum(kinds)])
    w_ref, keep_ref, send_ref, stack = refs[sum(kinds) :]
    requests, tokens, _ = xs[0].shape
    half = sections * tokens
    section, rank = place_ref[0], place_ref[1]
    inner = (section > 0) & (section < sections - 1)
    for d, kind in enumerate(kinds):
        step = jnp.bitwise_xor(jnp.bitwise_xor(section, d), rank // 2)

        def put(x):
            for r in range(requests):
                base = pl.multiple_of((jnp.bitwise_xor(rank & 1, r) * sections + step) * tokens, tokens)
                stack[pl.ds(base, tokens)] = x[r]

        if kind == 1:
            put(xs.pop(0))
        else:
            pl.when(inner)(partial(put, xs.pop(0)))
            pl.when(jnp.logical_not(inner))(partial(put, xs.pop(0)))

    def columns(j, _):
        at = pl.ds(pl.multiple_of(j * width, width), width)
        taken = pl.ds(pl.multiple_of(start + j * width, width), width)
        out = jnp.dot(stack[...], w_ref[:, taken], preferred_element_type=f32)
        keep_ref[:, :, at] = out[:half].reshape(sections, tokens, width).astype(keep_ref.dtype)
        send_ref[:, :, at] = out[half:].reshape(sections, tokens, width).astype(send_ref.dtype)
        return 0

    lax.fori_loop(0, keep_ref.shape[2] // width, columns, 0)


def project(place, blocks, weight, start, columns, width=2048):
    width = min(width, columns)
    assert columns % width == 0 and start % width == 0
    sections = len(blocks)
    kinds = tuple(len(block) for block in blocks)
    flat = [x for block in blocks for x in block]
    requests, tokens, features = flat[0].shape
    vmem = pl.BlockSpec(memory_space=pltpu.VMEM)
    return pl.pallas_call(
        partial(project_kernel, kinds=kinds, width=width, start=start),
        in_specs=[pl.BlockSpec(memory_space=pltpu.SMEM)] + [vmem] * (len(flat) + 1),
        out_specs=[vmem, vmem],
        out_shape=[
            jax.ShapeDtypeStruct((sections, tokens, columns), f32),
            jax.ShapeDtypeStruct((sections, tokens, columns), bf16),
        ],
        scratch_shapes=[pltpu.VMEM((sections * requests * tokens, features), bf16)],
        compiler_params=pltpu.CompilerParams(vmem_limit_bytes=16 << 20),
        cost_estimate=pl.CostEstimate(
            flops=2 * sections * requests * tokens * features * columns,
            transcendentals=0,
            bytes_accessed=features * columns * 2 + sections * requests * tokens * (features + columns) * 2,
        ),
        name="project",
    )(place, *flat, weight)


def merge_kernel(keep_ref, partner_ref, own_ref, *send_refs):
    for d in range(keep_ref.shape[0]):
        both = keep_ref[d] + partner_ref[d].astype(f32)
        if d == 0:
            own_ref[...] = both
        else:
            send_refs[d - 1][...] = both.astype(bf16)


def merge(keep, partner):
    vmem = pl.BlockSpec(memory_space=pltpu.VMEM)
    count, tokens, columns = keep.shape
    return pl.pallas_call(
        merge_kernel,
        in_specs=[vmem] * 2,
        out_specs=[vmem] * count,
        out_shape=[jax.ShapeDtypeStruct((tokens, columns), f32)]
        + [jax.ShapeDtypeStruct((tokens, columns), bf16)] * (count - 1),
        compiler_params=pltpu.CompilerParams(vmem_limit_bytes=12 << 20),
        name="merge",
    )(keep, partner)


def finish_kernel(*refs, count, corners):
    *ins, out_ref = refs
    for g, (row, column) in enumerate(corners):
        total = ins[g * count][...]
        for ref in ins[g * count + 1 : (g + 1) * count]:
            total = total + ref[...].astype(f32)
        tokens, columns = total.shape
        out_ref[row : row + tokens, column : column + columns] = total


def finish(groups, corners, shape):
    vmem = pl.BlockSpec(memory_space=pltpu.VMEM)
    flat = [x for group in groups for x in group]
    return pl.pallas_call(
        partial(finish_kernel, count=len(groups[0]), corners=corners),
        in_specs=[vmem] * len(flat),
        out_specs=vmem,
        out_shape=jax.ShapeDtypeStruct(shape, f32),
        compiler_params=pltpu.CompilerParams(vmem_limit_bytes=12 << 20),
        name="finish",
    )(*flat)


def pairs(size, distance):
    return [(i, i ^ distance) for i in range(size)]


def shards(queries, tree_kv, cache, cache_len, parents, out_weight):
    requests, kv_count, _, _, hd = cache.shape
    tree = parents.shape[1]
    sections = lax.axis_size("section")
    ranks = lax.axis_size("tensor")
    chips = ranks // 2
    own_heads = queries.shape[1] // hd
    group = own_heads * ranks // kv_count
    scale = LOG2E / math.sqrt(hd)
    tokens = tree // CHUNKS
    held = kv_count // 2 if ranks == kv_count else kv_count
    assert requests == 2 and sections == chips == held and group % own_heads == 0
    place = jnp.stack([lax.axis_index("section"), lax.axis_index("tensor")]).astype(jnp.int32)

    def send(x, axis, size, distance, only=None):
        return lax.ppermute(x, axis, only or pairs(size, distance))

    def along(h, x):
        if sections != 4 or h > 0:
            return [[x]] + [[send(x, "section", sections, d)] for d in range(1, sections)]
        near = send(x, "section", sections, 1)
        middle = send(x, "section", sections, 3, [(1, 2), (2, 1)])
        crossed = send(near, "section", sections, 3, [(1, 2), (2, 1)])
        farthest = send(near, "section", sections, 2, [(1, 3), (2, 0)])
        passed = send(middle, "section", sections, 1, [(1, 0), (2, 3)])
        return [[x], [near], [crossed, passed], [middle, farthest]]

    cache = pltpu.with_memory_space_constraint(cache, pltpu.HBM)
    sending = stage(place, cache, held)
    got = send(sending, "tensor", ranks, 1)
    queries = queries.reshape(requests, tree, queries.shape[1])
    asked = []
    for h in range(CHUNKS):
        mine = queries[:, h * tokens : (h + 1) * tokens]
        direct = range(1, chips - 1 if chips == 4 else chips)
        asked.append([mine] + [send(mine, "tensor", ranks, 2 * d) for d in direct])
        if chips == 4:
            via = 1 + h % 2
            asked[h].append(send(asked[h][via], "tensor", ranks, 2 * (3 - via)))
    bias, tree_k, tree_v, dead, own = prep(
        place, cache_len, parents, tree_kv, cache, held, group // own_heads
    )
    weight = pltpu.with_memory_space_constraint(out_weight, pltpu.VMEM)

    gathered = []
    for h in range(CHUNKS):
        parts = []
        for d in range(chips):
            tree_args = () if d else (tree_k, tree_v, bias)
            part = attend(place, dead, asked[h][d], own, got, d, scale, h * tokens, tree_args)
            parts.append(send(part, "tensor", ranks, 2 * d) if d else part)
        attended = combine(parts, tokens)
        gathered.append(along(h, attended))
    groups, corners = [], []
    width = out_weight.shape[1]
    for h in range(CHUNKS):
        columns = width // PIECES[h]
        for c in range(PIECES[h]):
            keep, give = project(place, gathered[h], weight, c * columns, columns)
            partner = send(give, "tensor", ranks, 1)
            mine, *sends = merge(keep, partner)
            groups.append([mine] + [send(x, "tensor", ranks, 2 * (d + 1)) for d, x in enumerate(sends)])
            corners.append((h * tokens, c * columns))
    return finish(groups, tuple(corners), (CHUNKS * tokens, width))


def solution(mesh):
    in_specs = (
        P("section", "tensor"),
        P("section", None, None),
        P("section", None, None, "tensor", None),
        P("section"),
        P("section", None),
        P("tensor", "section"),
    )
    out_specs = P("tensor", "section")
    return jax.shard_map(shards, mesh=mesh, in_specs=in_specs, out_specs=out_specs, check_vma=False)
```
